256 devices in a mesh: wave: 32 (over z, y), lev: 8 (over x, core).
Axes of the slice: x: 4, y: 4, z: 8, core: 2. Of those that a mesh axis runs over, the one named last changes fastest.
Arguments:
- fourier: bfloat16 [2560, 128, 4, 128], P('wave', 'lev'), may hold values from -6 to 6
- owner: int32 [64], replicated, may hold values from 0 to 63, each once
- legendre: bfloat16 [64, 2, 640, 1280], P('wave'), may hold values from -0.125 to 0.125
- quad_weights: float32 [1280], replicated, may hold values from 0.5 to 2
- layer_depth: float32 [128], P('lev'), may hold values from 0.05 to 0.3
Outputs:
- fields_out: bfloat16 [2560, 128, 4, 128], P('wave', 'lev')
- geopotential: bfloat16 [2560, 128, 128], P('wave', 'lev')
The draws below stay inside these ranges and needn't reach their ends.
Inputs may be any that keep to these rules, and one draw needn't show every extreme that they name: owner is a permutation of the slots; slot s lies on index s // 2 of wave.
All inputs are finite; a program needn't handle non-finite values.
Results may differ from the reference program's by a relative error of at most 0.0063.
Values may be sent and summed in bfloat16 or wider, within the bound.
No kernel may reach another device: no remote copies, remote signals or barrier semaphores. Data moves between devices by JAX's collectives and lax.ppermute only.
A program may use at most 64 MiB of HBM per device.

```python
import math
import jax
import jax.numpy as jnp
from jax import lax

NMAX = 1280
NLATH = 1280
FIELDS = 4
LEV = 128
MW = 64
NLAT = 2560
HALF = 640


def shard_levels(rng, dims, split, smallest, top_value):
    gain, own = 1.0, jax.random.fold_in(rng, 6)
    for position, blocks in split:
        heights = jnp.exp(jax.random.uniform(jax.random.fold_in(own, position), (blocks,), jnp.float32, smallest / len(split), top_value / len(split)))
        gain = gain * jnp.repeat(heights, dims[position] // blocks).reshape([-1 if axis == position else 1 for axis in range(len(dims))])
    return gain


def gaussian(own_key, extent, width, bound, cuts=(), kind=jnp.bfloat16):
    entries = jax.random.normal(own_key, extent, jnp.float32) * width
    if len(cuts) > 0:
        entries = shard_levels(own_key, extent, cuts, -0.22, 0.18) * entries
    return jnp.clip(entries, min=-bound, max=bound).astype(kind)


def setup_inputs(seed: int = 0) -> dict:
    seeds = jax.random.split(jax.random.key(seed), 6)
    fourier = gaussian(seeds[0], (NLAT, LEV, FIELDS, 2 * MW), 1.0, 6.0, ((0, 32), (1, 8)))
    owner = jax.random.permutation(seeds[1], MW).astype(jnp.int32)
    legendre = gaussian(seeds[2], (MW, 2, HALF, NLATH), NLAT ** -0.5, 0.125, ((0, 32),))
    quad_weights = jnp.clip(jnp.exp(jax.random.uniform(seeds[3], (NLATH,), jnp.float32, math.log(0.5), math.log(2.0))), 0.5, 2.0)
    layer_depth = jnp.clip(jnp.exp(math.log(0.3) - 1.7917595 * jax.random.uniform(seeds[4], (LEV,), jnp.float32) ** shard_levels(seeds[4], (LEV,), ((0, 8),), -0.2, 0.2)), 0.05, 0.3)
    return dict(fourier=fourier, owner=owner, legendre=legendre, quad_weights=quad_weights, layer_depth=layer_depth)


def reference(fourier, owner, legendre, quad_weights, layer_depth):
    unpacked = fourier.reshape(NLAT, LEV, FIELDS, 2, MW)
    columns_all = jnp.transpose(unpacked, (4, 0, 1, 2, 3)).reshape(MW, NLAT, LEV * FIELDS * 2)
    degree_rows = jnp.arange(HALF, dtype=jnp.int32)

    def transform(inputs):
        wave_index, columns = inputs
        tables = legendre[owner[wave_index]]
        length = NMAX - (wave_index * NMAX) // MW
        values = columns.astype(jnp.float32)
        northern = values[:NLATH]
        southern = values[NLATH:][::-1]
        scaled = quad_weights[:, None]
        folded = ((scaled * (northern + southern)).astype(jnp.bfloat16),
                  (scaled * (northern - southern)).astype(jnp.bfloat16))
        halves = []
        for parity in range(2):
            spectra = jnp.dot(tables[parity], folded[parity], preferred_element_type=jnp.float32)
            living = (2 * degree_rows + parity) < length
            spectra = jnp.where(living[:, None], spectra, jnp.float32(0.0)).astype(jnp.bfloat16)
            halves.append(jnp.dot(tables[parity].T, spectra, preferred_element_type=jnp.float32))
        upper = halves[0] + halves[1]
        lower = halves[0] - halves[1]
        return jnp.concatenate([upper, lower[::-1]], axis=0).astype(jnp.bfloat16)

    results = lax.map(transform, (jnp.arange(MW, dtype=jnp.int32), columns_all))
    fields_out = jnp.transpose(results.reshape(MW, NLAT, LEV, FIELDS, 2), (1, 2, 3, 4, 0)).reshape(NLAT, LEV, FIELDS, 2 * MW)
    contrib = layer_depth[None, :, None] * fields_out[:, :, 0, :].astype(jnp.float32)
    inclusive = jnp.cumsum(contrib[:, ::-1], axis=1)[:, ::-1]
    geopotential = (inclusive - 0.5 * contrib).astype(jnp.bfloat16)
    return fields_out, geopotential
```

```python
import jax
import jax.numpy as jnp
from jax import lax
from jax.experimental import pallas as pl
from jax.experimental.pallas import tpu as pltpu
from jax.sharding import PartitionSpec as P

F32 = jnp.float32
BF16 = jnp.bfloat16
NT = (((1,), (1,)), ((), ()))
NN = (((1,), (0,)), ((), ()))
VMEM = pl.BlockSpec(memory_space=pltpu.VMEM)
SMEM = pl.BlockSpec(memory_space=pltpu.SMEM)
ANY = pl.BlockSpec(memory_space=pl.ANY)


def dot(a, b, dims):
    return lax.dot_general(a, b, dims, preferred_element_type=F32)


def identity(size):
    rows = lax.broadcasted_iota(jnp.int32, (size, size), 0)
    cols = lax.broadcasted_iota(jnp.int32, (size, size), 1)
    return jnp.where(rows == cols, 1.0, 0.0).astype(BF16)


def regroup(first, second):
    lanes = first.shape[1]
    half = lanes // 2
    low = lax.broadcasted_iota(jnp.int32, first.shape, 1) < half
    return (
        jnp.where(low, first, pltpu.roll(second, half, 1)),
        jnp.where(low, pltpu.roll(first, half, 1), second),
    )


def pack_kernel(owner_ref, flip_ref, x_ref, out_ref, spread):
    waves, lat_rows, lanes = out_ref.shape
    eye = identity(lanes)
    flip = flip_ref[0]

    def pair(turn, _):
        rows = x_ref[pl.ds(turn * lanes, lanes), :]
        turned = dot(eye, rows, NT)
        tiles = regroup(turned[:waves], turned[waves:])
        for step, tile in enumerate(tiles):
            lat = 2 * turn + step
            place = jnp.where(flip > 0, lat_rows - 1 - lat, lat)
            spread[pl.ds(place, waves, stride=lat_rows), :] = tile
        return 0

    lax.fori_loop(0, lat_rows // 2, pair, 0, unroll=4)

    def slot(wave, _):
        out_ref[owner_ref[wave]] = spread[pl.ds(wave * lat_rows, lat_rows), :].astype(BF16)
        return 0

    lax.fori_loop(0, waves, slot, 0, unroll=4)


def pack(x, owner, flip):
    lat_rows, level_count, field_count, lanes = x.shape
    waves = lanes // 2
    return pl.pallas_call(
        pack_kernel,
        out_shape=jax.ShapeDtypeStruct((waves, lat_rows, lanes), BF16),
        in_specs=[SMEM, SMEM, VMEM],
        out_specs=VMEM,
        scratch_shapes=[pltpu.VMEM((waves * lat_rows, lanes), F32)],
        name="pack",
    )(owner, flip, x.reshape(lat_rows * level_count * field_count, lanes))


def legendre_kernel(length_ref, weight_ref, x_ref, table_hbm, out_ref, table, folded, sems):
    blocks, slots, lat_rows, lanes = x_ref.shape
    half_blocks = blocks // 2
    rows, half_lats = table.shape[2:]
    copies = []
    for slot in range(slots):
        for parity in range(2):
            copy = pltpu.make_async_copy(
                table_hbm.at[slot, parity], table.at[slot, parity], sems.at[slot, parity]
            )
            copy.start()
            copies.append(copy)
    for slot in range(slots):
        for block in range(half_blocks):
            span = pl.ds(block * lat_rows, lat_rows)
            north = x_ref[block, slot].astype(F32)
            south = x_ref[blocks - 1 - block, slot].astype(F32)
            weight = weight_ref[span, :]
            folded[0, span, :] = (weight * (north + south)).astype(BF16)
            folded[1, span, :] = (weight * (north - south)).astype(BF16)
        parts = []
        for parity in range(2):
            copies[slot * 2 + parity].wait()
            spectra = dot(table[slot, parity], folded[parity], NN)
            degree = 2 * lax.broadcasted_iota(jnp.int32, spectra.shape, 0) + parity
            spectra = jnp.where(degree < length_ref[slot], spectra, 0.0)
            parts.append(dot(spectra.T.astype(BF16), table[slot, parity], NN))
        upper = (parts[0] + parts[1]).T.astype(BF16)
        lower = (parts[0] - parts[1]).T.astype(BF16)
        for block in range(half_blocks):
            span = slice(block * lat_rows, (block + 1) * lat_rows)
            out_ref[block, slot] = upper[span]
            out_ref[blocks - 1 - block, slot] = lower[span]


def legendre_pair(x, table, weight, length):
    half_lats, lanes = weight.shape
    return pl.pallas_call(
        legendre_kernel,
        out_shape=jax.ShapeDtypeStruct(x.shape, BF16),
        in_specs=[SMEM, VMEM, VMEM, ANY],
        out_specs=VMEM,
        scratch_shapes=[
            pltpu.VMEM(table.shape, BF16),
            pltpu.VMEM((2, half_lats, lanes), BF16),
            pltpu.SemaphoreType.DMA((table.shape[0], 2)),
        ],
        name="legendre",
    )(length, weight, x, table)


def unpack_kernel(owner_ref, flip_ref, mix_ref, x_ref, out_ref, geo_ref, total_ref, spread):
    waves, lat_rows, lanes = x_ref.shape
    levels = geo_ref.shape[1]
    flip = flip_ref[0]

    def slot(wave, _):
        spread[pl.ds(wave * lat_rows, lat_rows), :] = x_ref[owner_ref[wave]].astype(F32)
        return 0

    lax.fori_loop(0, waves, slot, 0, unroll=4)
    mix = mix_ref[...]

    def pair(turn, _):
        tiles = []
        for step in range(2):
            lat = 2 * turn + step
            place = jnp.where(flip > 0, lat_rows - 1 - lat, lat)
            tiles.append(spread[pl.ds(place, waves, stride=lat_rows), :])
        rows = jnp.concatenate(tiles, axis=0).astype(BF16)
        turned = dot(mix, rows, NT)
        for step, tile in enumerate(regroup(turned[:waves], turned[waves : 2 * waves])):
            out_ref[2 * turn + step] = tile.astype(BF16)
        sums = turned[lanes : lanes + 48] + turned[lanes + 48 : lanes + 96]
        for step, tile in enumerate(regroup(sums[:24], sums[24:])):
            geo_ref[2 * turn + step] = tile[:levels]
            total_ref[pl.ds(2 * turn + step, 1), :] = tile[levels : levels + 1]
        return 0

    lax.fori_loop(0, lat_rows // 2, pair, 0, unroll=4)


def unpack(x, owner, flip, mix, levels):
    waves, lat_rows, lanes = x.shape
    return pl.pallas_call(
        unpack_kernel,
        out_shape=(
            jax.ShapeDtypeStruct((lat_rows, waves, lanes), BF16),
            jax.ShapeDtypeStruct((lat_rows, levels, lanes), F32),
            jax.ShapeDtypeStruct((lat_rows, lanes), F32),
        ),
        in_specs=[SMEM, SMEM, VMEM, VMEM],
        out_specs=(VMEM, VMEM, VMEM),
        scratch_shapes=[pltpu.VMEM((waves * lat_rows, lanes), F32)],
        name="unpack",
    )(owner, flip, mix, x)


def mixing(layer_depth, field_count):
    levels = layer_depth.shape[0]
    columns = levels * field_count
    to = jnp.arange(24)[:, None]
    column = jnp.arange(columns)[None, :]
    level = column // field_count
    share = jnp.where(to == level, 0.5, jnp.where(to < level, 1.0, 0.0))
    share = jnp.where(to == levels, 1.0, jnp.where(to > levels, 0.0, share))
    share = jnp.where(column % field_count == 0, share, 0.0)
    weight = share * jnp.repeat(layer_depth, field_count)[None, :]
    high = weight.astype(BF16)
    low = (weight - high.astype(F32)).astype(BF16)
    blank = jnp.zeros_like(high)
    both = [
        jnp.concatenate(pieces, axis=1)
        for pieces in ((high, blank), (blank, high), (low, blank), (blank, low))
    ]
    return jnp.concatenate([jnp.eye(2 * columns, dtype=BF16)] + both, axis=0)


def on_device(fourier, owner, legendre, quad_weights, layer_depth):
    lat_rows, level_count, field_count, doubled = fourier.shape
    waves = doubled // 2
    slots = legendre.shape[0]
    degrees = 2 * legendre.shape[2]
    blocks = waves // slots
    place = lax.axis_index("wave")
    flip = (place >= blocks // 2).astype(jnp.int32).reshape(1)
    mine = place * slots + jnp.arange(slots, dtype=jnp.int32)
    wave_ids = jnp.arange(waves, dtype=jnp.int32)
    my_waves = jnp.sum(jnp.where(owner[None, :] == mine[:, None], wave_ids[None, :], 0), axis=1)
    lengths = degrees - my_waves * degrees // waves
    weight = jnp.broadcast_to(quad_weights[:, None], (quad_weights.shape[0], doubled))
    mix = mixing(layer_depth, field_count)

    outgoing = pack(fourier, owner, flip)
    arrived = lax.all_to_all(outgoing, "wave", split_axis=0, concat_axis=0, tiled=True)
    arrived = arrived.reshape(blocks, slots, lat_rows, doubled)
    results = legendre_pair(arrived, legendre, weight, lengths)
    results = results.reshape(waves, lat_rows, doubled)
    returned = lax.all_to_all(results, "wave", split_axis=0, concat_axis=0, tiled=True)
    fields, inside, total = unpack(returned, owner, flip, mix, level_count)
    fields_out = fields.reshape(fourier.shape)
    gathered = lax.all_gather(total, "lev")
    lev = lax.axis_index("lev")
    later = jnp.arange(gathered.shape[0], dtype=jnp.int32) > lev
    below = jnp.sum(jnp.where(later[:, None, None], gathered, 0.0), axis=0)
    geopotential = (below[:, None, :] + inside).astype(BF16)
    return (fields_out, geopotential)


def solution(mesh):
    return jax.shard_map(
        on_device,
        mesh=mesh,
        in_specs=(P("wave", "lev", None, None), P(), P("wave", None, None, None), P(), P("lev")),
        out_specs=(P("wave", "lev", None, None), P("wave", "lev", None)),
        check_vma=False,
    )
```

```python
import jax
import jax.numpy as jnp
from jax import lax
from jax.experimental import pallas as pl
from jax.experimental.pallas import tpu as pltpu
from jax.sharding import PartitionSpec as P

F32 = jnp.float32
BF16 = jnp.bfloat16
MIB = 1 << 20
PAD = 8
NT = (((1,), (1,)), ((), ()))
NN = (((1,), (0,)), ((), ()))
VMEM = pl.BlockSpec(memory_space=pltpu.VMEM)
SMEM = pl.BlockSpec(memory_space=pltpu.SMEM)
ANY = pl.BlockSpec(memory_space=pl.ANY)
HBM = pl.BlockSpec(memory_space=pltpu.HBM)


def dot(a, b, dims):
    return lax.dot_general(a, b, dims, preferred_element_type=F32)


def identity(size):
    rows = lax.broadcasted_iota(jnp.int32, (size, size), 0)
    cols = lax.broadcasted_iota(jnp.int32, (size, size), 1)
    return jnp.where(rows == cols, 1.0, 0.0).astype(BF16)


def regroup(first, second):
    half = first.shape[1] // 2
    return jnp.concatenate(
        [
            jnp.concatenate([first[:, :half], second[:, :half]], axis=1),
            jnp.concatenate([first[:, half:], second[:, half:]], axis=1),
        ],
        axis=0,
    )


def pack_kernel(owner_ref, flip_ref, x_ref, out_ref, spread):
    waves, lat_rows, lanes = out_ref.shape
    eye = identity(lanes)
    flip = flip_ref[0]
    for turn in range(lat_rows // 4):
        rows = [x_ref[lat * waves : (lat + 1) * waves, :] for lat in range(4 * turn, 4 * turn + 4)]
        both = jnp.concatenate([regroup(*rows[:2]), regroup(*rows[2:])], axis=0)
        turned = dot(eye, both, NT)
        for step in range(4):
            row, column = step % 2 * waves, step // 2 * lanes
            lat = 4 * turn + step
            place = jnp.where(flip > 0, lat_rows - 1 - lat, lat)
            tile = turned[row : row + waves, column : column + lanes]
            spread[pl.ds(place, waves, stride=lat_rows + PAD), :] = tile
    for wave in range(waves):
        span = pl.ds(wave * (lat_rows + PAD), lat_rows)
        out_ref[owner_ref[wave]] = spread[span, :].astype(BF16)


def pack(x, owner, flip):
    lat_rows, level_count, field_count, lanes = x.shape
    waves = lanes // 2
    rows = lat_rows * level_count * field_count
    return pl.pallas_call(
        pack_kernel,
        out_shape=jax.ShapeDtypeStruct((waves, lat_rows, lanes), BF16),
        in_specs=[SMEM, SMEM, VMEM],
        out_specs=VMEM,
        scratch_shapes=[pltpu.VMEM((waves * (lat_rows + PAD), lanes), F32)],
        name="pack",
    )(owner, flip, x.reshape(rows, lanes))


def legendre_kernel(
    length_ref, weight_ref, x_ref, table_hbm, out_hbm, table, out_ref, folded, sems_in, sems_out
):
    blocks, slots, lat_rows, lanes = x_ref.shape
    half_blocks = blocks // 2

    def load(slot):
        return pltpu.make_async_copy(table_hbm.at[slot], table.at[slot], sems_in.at[slot])

    def store(slot):
        return pltpu.make_async_copy(out_ref.at[slot], out_hbm.at[:, slot], sems_out.at[slot])

    for slot in range(slots):
        load(slot).start()
    for slot in range(slots):
        for block in range(half_blocks):
            span = pl.ds(block * lat_rows, lat_rows)
            north = x_ref[block, slot].astype(F32)
            south = x_ref[blocks - 1 - block, slot].astype(F32)
            weight = weight_ref[span, :]
            folded[slot, 0, span, :] = (weight * (north + south)).astype(BF16)
            folded[slot, 1, span, :] = (weight * (north - south)).astype(BF16)
    for slot in range(slots):
        load(slot).wait()
        spectra = [dot(table[slot, parity], folded[slot, parity], NN) for parity in range(2)]
        turned = []
        for parity in range(2):
            degree = 2 * lax.broadcasted_iota(jnp.int32, spectra[parity].shape, 0) + parity
            live = jnp.where(degree < length_ref[slot], spectra[parity], 0.0)
            turned.append(live.T.astype(BF16))
        parts = [dot(turned[parity], table[slot, parity], NN) for parity in range(2)]
        upper = (parts[0] + parts[1]).T.astype(BF16)
        lower = (parts[0] - parts[1]).T.astype(BF16)
        for block in range(half_blocks):
            span = slice(block * lat_rows, (block + 1) * lat_rows)
            out_ref[slot, block] = upper[span]
            out_ref[slot, blocks - 1 - block] = lower[span]
        store(slot).start()
    for slot in range(slots):
        store(slot).wait()


def legendre_pair(x, table, weight, length):
    half_lats, lanes = weight.shape
    blocks, slots, lat_rows, lanes = x.shape
    return pl.pallas_call(
        legendre_kernel,
        out_shape=jax.ShapeDtypeStruct(x.shape, BF16),
        in_specs=[SMEM, VMEM, VMEM, HBM],
        out_specs=HBM,
        scratch_shapes=[
            pltpu.VMEM(table.shape, BF16),
            pltpu.VMEM((slots, blocks, lat_rows, lanes), BF16),
            pltpu.VMEM((slots, 2, half_lats, lanes), BF16),
            pltpu.SemaphoreType.DMA((slots,)),
            pltpu.SemaphoreType.DMA((slots,)),
        ],
        name="legendre",
        compiler_params=pltpu.CompilerParams(vmem_limit_bytes=50 * MIB),
    )(length, weight, x, table)


def totals_kernel(owner_ref, sum_ref, x_ref, out_ref, lines):
    waves, lat_rows, lanes = x_ref.shape
    weight = sum_ref[...]
    lines[...] = jnp.zeros_like(lines)
    for wave in range(waves):
        line = dot(weight, x_ref[owner_ref[wave]], NT)
        line = line[0:2] + line[2:4]
        lines[wave : wave + 1, :lat_rows] = line[0:1]
        lines[waves + wave : waves + wave + 1, :lat_rows] = line[1:2]
    out_ref[...] = lines[...].T[:lat_rows]


def totals(x, owner, weight):
    waves, lat_rows, lanes = x.shape
    return pl.pallas_call(
        totals_kernel,
        out_shape=jax.ShapeDtypeStruct((lat_rows, lanes), F32),
        in_specs=[SMEM, VMEM, VMEM],
        out_specs=VMEM,
        scratch_shapes=[pltpu.VMEM((lanes, lanes), F32)],
        name="totals",
        compiler_params=pltpu.CompilerParams(vmem_limit_bytes=6 * MIB),
    )(owner, weight, x)


def unpack_kernel(owner_ref, flip_ref, mix_ref, x_ref, out_hbm, geo_ref, out_ref, spread, sems):
    waves, lat_rows, lanes = x_ref.shape
    levels = geo_ref.shape[1]
    flip = flip_ref[0]
    parts = sems.shape[0]
    quads = lat_rows // 4 // parts
    rows = waves + 2 * levels

    def store(part):
        span = pl.ds(part * 4 * quads, 4 * quads)
        return pltpu.make_async_copy(out_ref.at[span], out_hbm.at[span], sems.at[part])

    for wave in range(waves):
        span = pl.ds(wave * (lat_rows + PAD), lat_rows)
        spread[span, :] = x_ref[owner_ref[wave]].astype(F32)
    for part in range(parts):
        for turn in range(part * quads, (part + 1) * quads):
            tiles = []
            for step in range(4):
                lat = 4 * turn + step
                place = jnp.where(flip > 0, lat_rows - 1 - lat, lat)
                tiles.append(spread[pl.ds(place, waves, stride=lat_rows + PAD), :].astype(BF16))
            both = jnp.concatenate([regroup(*tiles[:2]), regroup(*tiles[2:])], axis=0)
            turned = dot(mix_ref[...], both, NT)
            for step in range(4):
                lat = 4 * turn + step
                side = turned[:, step // 2 * lanes : (step // 2 + 1) * lanes]
                side = side[step % 2 * rows : (step % 2 + 1) * rows]
                out_ref[lat] = side[:waves].astype(BF16)
                geo_ref[lat] = side[waves : waves + levels] + side[waves + levels :]
        store(part).start()
    for part in range(parts):
        store(part).wait()


def unpack(x, owner, flip, mix, levels):
    waves, lat_rows, lanes = x.shape
    return pl.pallas_call(
        unpack_kernel,
        out_shape=(
            jax.ShapeDtypeStruct((lat_rows, waves, lanes), BF16),
            jax.ShapeDtypeStruct((lat_rows, levels, lanes), F32),
        ),
        in_specs=[SMEM, SMEM, VMEM, VMEM],
        out_specs=(HBM, VMEM),
        scratch_shapes=[
            pltpu.VMEM((lat_rows, waves, lanes), BF16),
            pltpu.VMEM((waves * (lat_rows + PAD), lanes), F32),
            pltpu.SemaphoreType.DMA((5,)),
        ],
        name="unpack",
        compiler_params=pltpu.CompilerParams(vmem_limit_bytes=12 * MIB),
    )(owner, flip, mix, x)


def finish_kernel(flip_ref, inside_ref, own_ref, *refs):
    *later_refs, out_ref, below = refs
    lat_rows = out_ref.shape[0]
    flip = flip_ref[0]
    state = jnp.where(flip_ref[1] % 2 == 0, own_ref[...], 0.0)
    for step, ref in enumerate(later_refs):
        ahead = flip_ref[1] // 2 + step + 1 <= len(later_refs)
        state = state + jnp.where(ahead, ref[...], 0.0)
    below[...] = state
    for lat in range(lat_rows):
        place = jnp.where(flip > 0, lat_rows - 1 - lat, lat)
        out_ref[lat] = (inside_ref[lat] + below[pl.ds(place, 1), :]).astype(BF16)


def finish(flags, inside, other, later):
    lat_rows, levels, lanes = inside.shape
    return pl.pallas_call(
        finish_kernel,
        out_shape=jax.ShapeDtypeStruct(inside.shape, BF16),
        in_specs=[SMEM] + [VMEM] * (2 + len(later)),
        out_specs=VMEM,
        scratch_shapes=[pltpu.VMEM((lat_rows, lanes), F32)],
        name="finish",
        compiler_params=pltpu.CompilerParams(vmem_limit_bytes=6 * MIB),
    )(flags, inside, other, *later)


def two_terms(weight):
    high = lax.reduce_precision(weight, 8, 7)
    return high.astype(BF16), (weight - high).astype(BF16)


def level_sums(layer_depth, field_count):
    levels = layer_depth.shape[0]
    columns = levels * field_count
    to = jnp.arange(levels)[:, None]
    column = jnp.arange(columns)[None, :]
    level = column // field_count
    depth = jnp.repeat(layer_depth, field_count)[None, :]
    depth = jnp.where(column % field_count == 0, depth, 0.0)
    share = jnp.where(to == level, 0.5, jnp.where(to < level, 1.0, 0.0))

    eye = jnp.eye(columns, dtype=BF16)
    inside = jnp.concatenate((eye,) + two_terms(share * depth), axis=0)
    blank = jnp.zeros_like(inside)
    mix = jnp.concatenate(
        [jnp.concatenate(pair, axis=1) for pair in ((inside, blank), (blank, inside))], axis=0
    )
    high, low = two_terms(depth)
    blank = jnp.zeros_like(high)
    pieces = ((high, blank), (blank, high), (low, blank), (blank, low))
    every = [jnp.concatenate(piece, axis=1) for piece in pieces]
    every = jnp.concatenate(every + [jnp.zeros((4, 2 * columns), BF16)], axis=0)
    return mix, every


def sums_of_later(total):
    count = lax.axis_size("lev")
    other = lax.ppermute(total, "lev", [(i, i ^ 1) for i in range(count)])
    both = total + other
    later = [
        lax.ppermute(both, "lev", [(i, (i - step) % count) for i in range(count)])
        for step in range(2, count, 2)
    ]
    return other, later


def on_device(fourier, owner, legendre, quad_weights, layer_depth):
    lat_rows, level_count, field_count, doubled = fourier.shape
    waves = doubled // 2
    slots = legendre.shape[0]
    degrees = 2 * legendre.shape[2]
    blocks = waves // slots
    place = lax.axis_index("wave")
    flip = (place >= blocks // 2).astype(jnp.int32).reshape(1)
    mine = place * slots + jnp.arange(slots, dtype=jnp.int32)
    wave_ids = jnp.arange(waves, dtype=jnp.int32)
    my_waves = jnp.sum(jnp.where(owner[None, :] == mine[:, None], wave_ids[None, :], 0), axis=1)
    lengths = degrees - my_waves * degrees // waves
    weight = jnp.broadcast_to(quad_weights[:, None], (quad_weights.shape[0], doubled))
    mix, every = level_sums(layer_depth, field_count)
    lev = lax.axis_index("lev").astype(jnp.int32).reshape(1)

    outgoing = pack(fourier, owner, flip)
    arrived = lax.all_to_all(outgoing, "wave", split_axis=0, concat_axis=0, tiled=True)
    arrived = arrived.reshape(blocks, slots, lat_rows, doubled)
    results = legendre_pair(arrived, legendre, weight, lengths)
    results = results.reshape(waves, lat_rows, doubled)
    returned = lax.all_to_all(results, "wave", split_axis=0, concat_axis=0, tiled=True)
    other, later = sums_of_later(totals(returned, owner, every))
    fields, inside = unpack(returned, owner, flip, mix, level_count)
    fields_out = fields.reshape(fourier.shape)
    geopotential = finish(jnp.concatenate([flip, lev]), inside, other, later)
    return (fields_out, geopotential)


def solution(mesh):
    return jax.shard_map(
        on_device,
        mesh=mesh,
        in_specs=(P("wave", "lev", None, None), P(), P("wave", None, None, None), P(), P("lev")),
        out_specs=(P("wave", "lev", None, None), P("wave", "lev", None)),
        check_vma=False,
    )
```

```python
import jax
import jax.numpy as jnp
from jax import lax
from jax.experimental import pallas as pl
from jax.experimental.pallas import tpu as pltpu
from jax.sharding import PartitionSpec as P

F32 = jnp.float32
BF16 = jnp.bfloat16
MIB = 1 << 20
PAD = 8
NT = (((1,), (1,)), ((), ()))
NN = (((1,), (0,)), ((), ()))
VMEM = pl.BlockSpec(memory_space=pltpu.VMEM)
SMEM = pl.BlockSpec(memory_space=pltpu.SMEM)
ANY = pl.BlockSpec(memory_space=pl.ANY)
HBM = pl.BlockSpec(memory_space=pltpu.HBM)


def dot(a, b, dims):
    return lax.dot_general(a, b, dims, preferred_element_type=F32)


def northern():
    return lax.axis_index("wave") < lax.axis_size("wave") // 2


def identity(size):
    rows = lax.broadcasted_iota(jnp.int32, (size, size), 0)
    cols = lax.broadcasted_iota(jnp.int32, (size, size), 1)
    return jnp.where(rows == cols, 1.0, 0.0).astype(BF16)


def regroup(first, second):
    half = first.shape[1] // 2
    return jnp.concatenate(
        [
            jnp.concatenate([first[:, :half], second[:, :half]], axis=1),
            jnp.concatenate([first[:, half:], second[:, half:]], axis=1),
        ],
        axis=0,
    )


def pack_kernel(
    owner_hbm, x_hbm, out_hbm, owner_ref, wave_of, x_ref, out_ref, spread, sems, sems_out
):
    waves, lat_rows, lanes = out_ref.shape
    first = lat_rows // 5 * waves
    spans = (pl.ds(0, first), pl.ds(first, lat_rows * waves - first))
    loads = [
        pltpu.make_async_copy(x_hbm.at[span], x_ref.at[span], sems.at[part])
        for part, span in enumerate(spans)
    ]
    loads.append(pltpu.make_async_copy(owner_hbm, owner_ref, sems.at[2]))
    for load in loads:
        load.start()
    eye = identity(lanes)
    north = northern()
    for turn in range(lat_rows // 4):
        if turn == 0:
            loads[0].wait()
        if 4 * turn * waves == first:
            loads[1].wait()
            loads[2].wait()
            for wave in range(waves):
                wave_of[owner_ref[wave]] = wave
        rows = [x_ref[lat * waves : (lat + 1) * waves, :] for lat in range(4 * turn, 4 * turn + 4)]
        both = jnp.concatenate([regroup(*rows[:2]), regroup(*rows[2:])], axis=0)
        turned = dot(eye, both, NT)
        for step in range(4):
            row, column = step % 2 * waves, step // 2 * lanes
            lat = 4 * turn + step
            place = jnp.where(north, lat, lat_rows - 1 - lat)
            tile = turned[row : row + waves, column : column + lanes]
            spread[pl.ds(place, waves, stride=lat_rows + PAD), :] = tile
    parts = sems_out.shape[0]
    size = waves // parts
    stores = []
    for part in range(parts):
        for slot in range(part * size, (part + 1) * size):
            start = pl.multiple_of(wave_of[slot] * (lat_rows + PAD), 8)
            out_ref[slot] = spread[pl.ds(start, lat_rows), :].astype(BF16)
        span = pl.ds(part * size, size)
        stores.append(
            pltpu.make_async_copy(out_ref.at[span], out_hbm.at[span], sems_out.at[part])
        )
        stores[-1].start()
    for store in stores:
        store.wait()


def pack(x, owner):
    lat_rows, level_count, field_count, lanes = x.shape
    waves = lanes // 2
    rows = lat_rows * level_count * field_count
    return pl.pallas_call(
        pack_kernel,
        out_shape=jax.ShapeDtypeStruct((waves, lat_rows, lanes), BF16),
        in_specs=[HBM, HBM],
        out_specs=HBM,
        scratch_shapes=[
            pltpu.SMEM((waves,), jnp.int32),
            pltpu.SMEM((waves,), jnp.int32),
            pltpu.VMEM((rows, lanes), BF16),
            pltpu.VMEM((waves, lat_rows, lanes), BF16),
            pltpu.VMEM(((waves + 1) * (lat_rows + PAD), lanes), F32),
            pltpu.SemaphoreType.DMA((3,)),
            pltpu.SemaphoreType.DMA((4,)),
        ],
        name="pack",
    )(owner, x.reshape(rows, lanes))


def legendre_kernel(
    weight_ref, x_ref, table_hbm, out_hbm, table, out_ref, folded, sems_in, sems_out
):
    blocks, slots, lat_rows, lanes = x_ref.shape
    half_blocks = blocks // 2

    def load(slot):
        return pltpu.make_async_copy(table_hbm.at[slot], table.at[slot], sems_in.at[slot])

    def store(slot):
        return pltpu.make_async_copy(out_ref.at[slot], out_hbm.at[:, slot], sems_out.at[slot])

    for slot in range(slots):
        load(slot).start()
    for slot in range(slots):
        for block in range(half_blocks):
            span = pl.ds(block * lat_rows, lat_rows)
            north = x_ref[block, slot].astype(F32)
            south = x_ref[blocks - 1 - block, slot].astype(F32)
            weight = weight_ref[span, :]
            folded[slot, 0, span, :] = (weight * (north + south)).astype(BF16)
            folded[slot, 1, span, :] = (weight * (north - south)).astype(BF16)
    def forward(slot):
        spectra = [dot(table[slot, parity], folded[slot, parity], NN) for parity in range(2)]
        row = half_blocks * lat_rows + slot
        length = weight_ref[row : row + 1, :]
        turned = []
        for parity in range(2):
            degree = 2 * lax.broadcasted_iota(jnp.int32, spectra[parity].shape, 0) + parity
            live = jnp.where(degree.astype(F32) < length, spectra[parity], 0.0)
            turned.append(live.T.astype(BF16))
        return turned

    def inverse(slot, turned):
        return [dot(turned[parity], table[slot, parity], NN) for parity in range(2)]

    def finish(slot, parts):
        upper = (parts[0] + parts[1]).T.astype(BF16)
        lower = (parts[0] - parts[1]).T.astype(BF16)
        for block in range(half_blocks):
            span = slice(block * lat_rows, (block + 1) * lat_rows)
            out_ref[slot, block] = upper[span]
            out_ref[slot, blocks - 1 - block] = lower[span]

    load(0).wait()
    turned = forward(0)
    load(1).wait()
    other = forward(1)
    finish(0, inverse(0, turned))
    store(0).start()
    finish(1, inverse(1, other))
    store(1).start()
    store(0).wait()
    store(1).wait()


def legendre_pair(x, table, weight):
    blocks, slots, lat_rows, lanes = x.shape
    half_lats = blocks // 2 * lat_rows
    return pl.pallas_call(
        legendre_kernel,
        out_shape=jax.ShapeDtypeStruct(x.shape, BF16),
        in_specs=[VMEM, VMEM, HBM],
        out_specs=HBM,
        scratch_shapes=[
            pltpu.VMEM(table.shape, BF16),
            pltpu.VMEM((slots, blocks, lat_rows, lanes), BF16),
            pltpu.VMEM((slots, 2, half_lats, lanes), BF16),
            pltpu.SemaphoreType.DMA((slots,)),
            pltpu.SemaphoreType.DMA((slots,)),
        ],
        name="legendre",
        compiler_params=pltpu.CompilerParams(vmem_limit_bytes=50 * MIB),
    )(weight, x, table)


def totals_kernel(owner_ref, sum_ref, x_ref, out_ref, lines):
    waves, lat_rows, lanes = x_ref.shape
    weight = sum_ref[...]
    lines[...] = jnp.zeros_like(lines)
    for wave in range(waves):
        line = dot(weight, x_ref[owner_ref[wave]], NT)
        line = line[0:2] + line[2:4]
        lines[wave : wave + 1, :lat_rows] = line[0:1]
        lines[waves + wave : waves + wave + 1, :lat_rows] = line[1:2]
    out_ref[...] = lines[...].T[:lat_rows]


def totals(x, owner, weight):
    waves, lat_rows, lanes = x.shape
    return pl.pallas_call(
        totals_kernel,
        out_shape=jax.ShapeDtypeStruct((lat_rows, lanes), F32),
        in_specs=[SMEM, VMEM, VMEM],
        out_specs=VMEM,
        scratch_shapes=[pltpu.VMEM((lanes, lanes), F32)],
        name="totals",
        compiler_params=pltpu.CompilerParams(vmem_limit_bytes=6 * MIB),
    )(owner, weight, x)


def unpack_kernel(owner_ref, mix_ref, x_ref, out_hbm, geo_ref, out_ref, spread, sems):
    waves, lat_rows, lanes = x_ref.shape
    levels = geo_ref.shape[1]
    north = northern()
    parts = sems.shape[0]
    quads = lat_rows // 4 // parts
    rows = waves + 2 * levels

    def store(part):
        span = pl.ds(part * 4 * quads, 4 * quads)
        return pltpu.make_async_copy(out_ref.at[span], out_hbm.at[span], sems.at[part])

    for wave in range(waves):
        span = pl.ds(wave * (lat_rows + PAD), lat_rows)
        spread[span, :] = x_ref[owner_ref[wave]].astype(F32)
    for part in range(parts):
        for turn in range(part * quads, (part + 1) * quads):
            tiles = []
            for step in range(4):
                lat = 4 * turn + step
                place = jnp.where(north, lat, lat_rows - 1 - lat)
                tiles.append(spread[pl.ds(place, waves, stride=lat_rows + PAD), :].astype(BF16))
            both = jnp.concatenate([regroup(*tiles[:2]), regroup(*tiles[2:])], axis=0)
            turned = dot(mix_ref[...], both, NT)
            for step in range(4):
                lat = 4 * turn + step
                side = turned[:, step // 2 * lanes : (step // 2 + 1) * lanes]
                side = side[step % 2 * rows : (step % 2 + 1) * rows]
                out_ref[lat] = side[:waves].astype(BF16)
                geo_ref[lat] = side[waves : waves + levels] + side[waves + levels :]
        store(part).start()
    for part in range(parts):
        store(part).wait()


def unpack(x, owner, mix, levels):
    waves, lat_rows, lanes = x.shape
    return pl.pallas_call(
        unpack_kernel,
        out_shape=(
            jax.ShapeDtypeStruct((lat_rows, waves, lanes), BF16),
            jax.ShapeDtypeStruct((lat_rows, levels, lanes), F32),
        ),
        in_specs=[SMEM, VMEM, VMEM],
        out_specs=(HBM, VMEM),
        scratch_shapes=[
            pltpu.VMEM((lat_rows, waves, lanes), BF16),
            pltpu.VMEM(((waves + 1) * (lat_rows + PAD), lanes), F32),
            pltpu.SemaphoreType.DMA((5,)),
        ],
        name="unpack",
        compiler_params=pltpu.CompilerParams(vmem_limit_bytes=12 * MIB),
    )(owner, mix, x)


def finish_kernel(inside_ref, own_ref, *refs):
    *later_refs, out_ref, below = refs
    lat_rows = out_ref.shape[0]
    north = northern()
    lev = lax.axis_index("lev")
    state = jnp.where(lev % 2 == 0, own_ref[...], 0.0)
    for step, ref in enumerate(later_refs):
        ahead = lev // 2 + step + 1 <= len(later_refs)
        state = state + jnp.where(ahead, ref[...], 0.0)
    below[...] = state
    for lat in range(lat_rows):
        place = jnp.where(north, lat, lat_rows - 1 - lat)
        out_ref[lat] = (inside_ref[lat] + below[pl.ds(place, 1), :]).astype(BF16)


def finish(inside, other, later):
    lat_rows, levels, lanes = inside.shape
    return pl.pallas_call(
        finish_kernel,
        out_shape=jax.ShapeDtypeStruct(inside.shape, BF16),
        in_specs=[VMEM] * (2 + len(later)),
        out_specs=VMEM,
        scratch_shapes=[pltpu.VMEM((lat_rows, lanes), F32)],
        name="finish",
        compiler_params=pltpu.CompilerParams(vmem_limit_bytes=6 * MIB),
    )(inside, other, *later)


def two_terms(weight):
    high = lax.reduce_precision(weight, 8, 7)
    return high.astype(BF16), (weight - high).astype(BF16)


def level_sums(layer_depth, field_count):
    levels = layer_depth.shape[0]
    columns = levels * field_count
    to = jnp.arange(levels)[:, None]
    column = jnp.arange(columns)[None, :]
    level = column // field_count
    depth = jnp.repeat(layer_depth, field_count)[None, :]
    depth = jnp.where(column % field_count == 0, depth, 0.0)
    share = jnp.where(to == level, 0.5, jnp.where(to < level, 1.0, 0.0))

    eye = jnp.eye(columns, dtype=BF16)
    inside = jnp.concatenate((eye,) + two_terms(share * depth), axis=0)
    blank = jnp.zeros_like(inside)
    mix = jnp.concatenate(
        [jnp.concatenate(pair, axis=1) for pair in ((inside, blank), (blank, inside))], axis=0
    )
    high, low = two_terms(depth)
    blank = jnp.zeros_like(high)
    pieces = ((high, blank), (blank, high), (low, blank), (blank, low))
    every = [jnp.concatenate(piece, axis=1) for piece in pieces]
    every = jnp.concatenate(every + [jnp.zeros((4, 2 * columns), BF16)], axis=0)
    return mix, every


def sums_of_later(total):
    count = lax.axis_size("lev")
    other = lax.ppermute(total, "lev", [(i, i ^ 1) for i in range(count)])
    both = total + other
    later = [
        lax.ppermute(both, "lev", [(i, (i - step) % count) for i in range(count)])
        for step in range(2, count, 2)
    ]
    return other, later


def on_device(fourier, owner, legendre, quad_weights, layer_depth):
    lat_rows, level_count, field_count, doubled = fourier.shape
    waves = doubled // 2
    slots = legendre.shape[0]
    degrees = 2 * legendre.shape[2]
    blocks = waves // slots
    place = lax.axis_index("wave")
    mine = place * slots + jnp.arange(slots, dtype=jnp.int32)
    wave_ids = jnp.arange(waves, dtype=jnp.int32)
    my_waves = jnp.sum(jnp.where(owner[None, :] == mine[:, None], wave_ids[None, :], 0), axis=1)
    lengths = degrees - my_waves * degrees // waves
    lines = jnp.concatenate([quad_weights, lengths.astype(F32), jnp.zeros((8 - slots,), F32)])
    weight = jnp.broadcast_to(lines[:, None], (lines.shape[0], doubled))
    mix, every = level_sums(layer_depth, field_count)

    outgoing = pack(fourier, owner)
    arrived = lax.all_to_all(outgoing, "wave", split_axis=0, concat_axis=0, tiled=True)
    arrived = arrived.reshape(blocks, slots, lat_rows, doubled)
    results = legendre_pair(arrived, legendre, weight)
    results = results.reshape(waves, lat_rows, doubled)
    returned = lax.all_to_all(results, "wave", split_axis=0, concat_axis=0, tiled=True)
    other, later = sums_of_later(totals(returned, owner, every))
    fields, inside = unpack(returned, owner, mix, level_count)
    fields_out = fields.reshape(fourier.shape)
    geopotential = finish(inside, other, later)
    return (fields_out, geopotential)


def solution(mesh):
    return jax.shard_map(
        on_device,
        mesh=mesh,
        in_specs=(P("wave", "lev", None, None), P(), P("wave", None, None, None), P(), P("lev")),
        out_specs=(P("wave", "lev", None, None), P("wave", "lev", None)),
        check_vma=False,
    )
```

```python
import jax
import jax.numpy as jnp
from jax import lax
from jax.experimental import pallas as pl
from jax.experimental.pallas import tpu as pltpu
from jax.sharding import PartitionSpec as P

F32 = jnp.float32
BF16 = jnp.bfloat16
MIB = 1 << 20
PAD = 8
NT = (((1,), (1,)), ((), ()))
NN = (((1,), (0,)), ((), ()))
VMEM = pl.BlockSpec(memory_space=pltpu.VMEM)
SMEM = pl.BlockSpec(memory_space=pltpu.SMEM)
ANY = pl.BlockSpec(memory_space=pl.ANY)
HBM = pl.BlockSpec(memory_space=pltpu.HBM)


def dot(a, b, dims):
    return lax.dot_general(a, b, dims, preferred_element_type=F32)


def northern():
    return lax.axis_index("wave") < lax.axis_size("wave") // 2


def identity(size):
    rows = lax.broadcasted_iota(jnp.int32, (size, size), 0)
    cols = lax.broadcasted_iota(jnp.int32, (size, size), 1)
    return jnp.where(rows == cols, 1.0, 0.0).astype(BF16)


def regroup(first, second):
    half = first.shape[1] // 2
    return jnp.concatenate(
        [
            jnp.concatenate([first[:, :half], second[:, :half]], axis=1),
            jnp.concatenate([first[:, half:], second[:, half:]], axis=1),
        ],
        axis=0,
    )


def pack_kernel(
    owner_hbm, x_hbm, out_hbm, owner_ref, wave_of, x_ref, out_ref, spread, sems, sems_out
):
    waves, lat_rows, lanes = out_ref.shape
    first = lat_rows // 5 * waves
    spans = (pl.ds(0, first), pl.ds(first, lat_rows * waves - first))
    loads = [
        pltpu.make_async_copy(x_hbm.at[span], x_ref.at[span], sems.at[part])
        for part, span in enumerate(spans)
    ]
    loads.append(pltpu.make_async_copy(owner_hbm, owner_ref, sems.at[2]))
    for load in loads:
        load.start()
    eye = identity(lanes)
    north = northern()
    for turn in range(lat_rows // 4):
        if turn == 0:
            loads[0].wait()
        if 4 * turn * waves == first:
            loads[1].wait()
            loads[2].wait()
            for wave in range(waves):
                wave_of[owner_ref[wave]] = wave
        rows = [x_ref[lat * waves : (lat + 1) * waves, :] for lat in range(4 * turn, 4 * turn + 4)]
        both = jnp.concatenate([regroup(*rows[:2]), regroup(*rows[2:])], axis=0)
        turned = dot(eye, both, NT)
        for step in range(4):
            row, column = step % 2 * waves, step // 2 * lanes
            lat = 4 * turn + step
            place = jnp.where(north, lat, lat_rows - 1 - lat)
            tile = turned[row : row + waves, column : column + lanes]
            spread[pl.ds(place, waves, stride=lat_rows + PAD), :] = tile
    parts = sems_out.shape[0]
    size = waves // parts
    stores = []
    for part in range(parts):
        for slot in range(part * size, (part + 1) * size):
            start = pl.multiple_of(wave_of[slot] * (lat_rows + PAD), 8)
            out_ref[slot] = spread[pl.ds(start, lat_rows), :].astype(BF16)
        span = pl.ds(part * size, size)
        stores.append(
            pltpu.make_async_copy(out_ref.at[span], out_hbm.at[span], sems_out.at[part])
        )
        stores[-1].start()
    for store in stores:
        store.wait()


def pack(x, owner):
    lat_rows, level_count, field_count, lanes = x.shape
    waves = lanes // 2
    rows = lat_rows * level_count * field_count
    return pl.pallas_call(
        pack_kernel,
        out_shape=jax.ShapeDtypeStruct((waves, lat_rows, lanes), BF16),
        in_specs=[HBM, HBM],
        out_specs=HBM,
        scratch_shapes=[
            pltpu.SMEM((waves,), jnp.int32),
            pltpu.SMEM((waves,), jnp.int32),
            pltpu.VMEM((rows, lanes), BF16),
            pltpu.VMEM((waves, lat_rows, lanes), BF16),
            pltpu.VMEM(((waves + 1) * (lat_rows + PAD), lanes), F32),
            pltpu.SemaphoreType.DMA((3,)),
            pltpu.SemaphoreType.DMA((4,)),
        ],
        name="pack",
    )(owner, x.reshape(rows, lanes))


def legendre_kernel(
    weight_ref, x_ref, table_hbm, out_hbm, table, out_ref, folded, sems_in, sems_out
):
    blocks, slots, lat_rows, lanes = x_ref.shape
    half_blocks = blocks // 2

    def load(slot):
        return pltpu.make_async_copy(table_hbm.at[slot], table.at[slot], sems_in.at[slot])

    def store(slot):
        return pltpu.make_async_copy(out_ref.at[slot], out_hbm.at[:, slot], sems_out.at[slot])

    for slot in range(slots):
        load(slot).start()
    for slot in range(slots):
        for block in range(half_blocks):
            span = pl.ds(block * lat_rows, lat_rows)
            north = x_ref[block, slot].astype(F32)
            south = x_ref[blocks - 1 - block, slot].astype(F32)
            weight = weight_ref[span, :]
            folded[slot, 0, span, :] = (weight * (north + south)).astype(BF16)
            folded[slot, 1, span, :] = (weight * (north - south)).astype(BF16)
    def forward(slot):
        spectra = [dot(table[slot, parity], folded[slot, parity], NN) for parity in range(2)]
        row = half_blocks * lat_rows + slot
        length = weight_ref[row : row + 1, :]
        turned = []
        for parity in range(2):
            degree = 2 * lax.broadcasted_iota(jnp.int32, spectra[parity].shape, 0) + parity
            live = jnp.where(degree.astype(F32) < length, spectra[parity], 0.0)
            turned.append(live.T.astype(BF16))
        return turned

    def inverse(slot, turned):
        return [dot(turned[parity], table[slot, parity], NN) for parity in range(2)]

    def finish(slot, parts):
        upper = (parts[0] + parts[1]).T.astype(BF16)
        lower = (parts[0] - parts[1]).T.astype(BF16)
        for block in range(half_blocks):
            span = slice(block * lat_rows, (block + 1) * lat_rows)
            out_ref[slot, block] = upper[span]
            out_ref[slot, blocks - 1 - block] = lower[span]

    load(0).wait()
    turned = forward(0)
    load(1).wait()
    other = forward(1)
    finish(0, inverse(0, turned))
    store(0).start()
    finish(1, inverse(1, other))
    store(1).start()
    store(0).wait()
    store(1).wait()


def legendre_pair(x, table, weight):
    blocks, slots, lat_rows, lanes = x.shape
    half_lats = blocks // 2 * lat_rows
    return pl.pallas_call(
        legendre_kernel,
        out_shape=jax.ShapeDtypeStruct(x.shape, BF16),
        in_specs=[VMEM, VMEM, HBM],
        out_specs=HBM,
        scratch_shapes=[
            pltpu.VMEM(table.shape, BF16),
            pltpu.VMEM((slots, blocks, lat_rows, lanes), BF16),
            pltpu.VMEM((slots, 2, half_lats, lanes), BF16),
            pltpu.SemaphoreType.DMA((slots,)),
            pltpu.SemaphoreType.DMA((slots,)),
        ],
        name="legendre",
        compiler_params=pltpu.CompilerParams(vmem_limit_bytes=50 * MIB),
    )(weight, x, table)


def totals_kernel(sum_ref, x_ref, out_ref):
    waves, lat_rows, lanes = x_ref.shape
    weight = sum_ref[...]
    lane = lax.broadcasted_iota(jnp.int32, (lat_rows, lanes), 1) % waves
    state = jnp.zeros((lat_rows, lanes), F32)
    for first in range(0, waves, 8):
        group = range(first, first + 8)
        rows = jnp.concatenate([x_ref[wave] for wave in group], axis=0)
        spread = dot(jnp.concatenate([rows, rows], axis=1), weight, NN)
        for step, wave in enumerate(group):
            side = spread[step * lat_rows : (step + 1) * lat_rows]
            state = jnp.where(lane == wave, side, state)
    out_ref[...] = state


def totals(x, weight):
    waves, lat_rows, lanes = x.shape
    return pl.pallas_call(
        totals_kernel,
        out_shape=jax.ShapeDtypeStruct((lat_rows, lanes), F32),
        in_specs=[VMEM, VMEM],
        out_specs=VMEM,
        name="totals",
        compiler_params=pltpu.CompilerParams(vmem_limit_bytes=6 * MIB),
    )(weight, x)


def unpack_kernel(owner_ref, mix_ref, x_ref, out_hbm, geo_ref, out_ref, spread, sems):
    waves, lat_rows, lanes = x_ref.shape
    levels = geo_ref.shape[1]
    north = northern()
    parts = sems.shape[0]
    quads = lat_rows // 4 // parts
    rows = waves + 2 * levels

    def store(part):
        span = pl.ds(part * 4 * quads, 4 * quads)
        return pltpu.make_async_copy(out_ref.at[span], out_hbm.at[span], sems.at[part])

    for wave in range(waves):
        span = pl.ds(wave * (lat_rows + PAD), lat_rows)
        spread[span, :] = x_ref[owner_ref[wave]].astype(F32)
    for part in range(parts):
        for turn in range(part * quads, (part + 1) * quads):
            tiles = []
            for step in range(4):
                lat = 4 * turn + step
                place = jnp.where(north, lat, lat_rows - 1 - lat)
                tiles.append(spread[pl.ds(place, waves, stride=lat_rows + PAD), :].astype(BF16))
            both = jnp.concatenate([regroup(*tiles[:2]), regroup(*tiles[2:])], axis=0)
            turned = dot(mix_ref[...], both, NT)
            for step in range(4):
                lat = 4 * turn + step
                side = turned[:, step // 2 * lanes : (step // 2 + 1) * lanes]
                side = side[step % 2 * rows : (step % 2 + 1) * rows]
                out_ref[lat] = side[:waves].astype(BF16)
                geo_ref[lat] = side[waves : waves + levels] + side[waves + levels :]
        store(part).start()
    for part in range(parts):
        store(part).wait()


def unpack(x, owner, mix, levels):
    waves, lat_rows, lanes = x.shape
    return pl.pallas_call(
        unpack_kernel,
        out_shape=(
            jax.ShapeDtypeStruct((lat_rows, waves, lanes), BF16),
            jax.ShapeDtypeStruct((lat_rows, levels, lanes), F32),
        ),
        in_specs=[SMEM, VMEM, VMEM],
        out_specs=(HBM, VMEM),
        scratch_shapes=[
            pltpu.VMEM((lat_rows, waves, lanes), BF16),
            pltpu.VMEM(((waves + 1) * (lat_rows + PAD), lanes), F32),
            pltpu.SemaphoreType.DMA((5,)),
        ],
        name="unpack",
        compiler_params=pltpu.CompilerParams(vmem_limit_bytes=12 * MIB),
    )(owner, mix, x)


def finish_kernel(order_ref, inside_ref, own_ref, *refs):
    *later_refs, out_ref, below = refs
    lat_rows = out_ref.shape[0]
    north = northern()
    lev = lax.axis_index("lev")
    state = jnp.where(lev % 2 == 0, own_ref[...], 0.0)
    for step, ref in enumerate(later_refs):
        ahead = lev // 2 + step + 1 <= len(later_refs)
        state = state + jnp.where(ahead, ref[...], 0.0)
    terms = []
    for _ in range(3):
        terms.append(state.astype(BF16))
        state = state - terms[-1].astype(F32)
    below[...] = sum(dot(term, order_ref[...], NN) for term in terms)
    for lat in range(lat_rows):
        place = jnp.where(north, lat, lat_rows - 1 - lat)
        out_ref[lat] = (inside_ref[lat] + below[pl.ds(place, 1), :]).astype(BF16)


def finish(order, inside, other, later):
    lat_rows, levels, lanes = inside.shape
    return pl.pallas_call(
        finish_kernel,
        out_shape=jax.ShapeDtypeStruct(inside.shape, BF16),
        in_specs=[VMEM] * (3 + len(later)),
        out_specs=VMEM,
        scratch_shapes=[pltpu.VMEM((lat_rows, lanes), F32)],
        name="finish",
        compiler_params=pltpu.CompilerParams(vmem_limit_bytes=6 * MIB),
    )(order, inside, other, *later)


def two_terms(weight):
    high = lax.reduce_precision(weight, 8, 7)
    return high.astype(BF16), (weight - high).astype(BF16)


def level_sums(layer_depth, field_count):
    levels = layer_depth.shape[0]
    columns = levels * field_count
    to = jnp.arange(levels)[:, None]
    column = jnp.arange(columns)[None, :]
    level = column // field_count
    depth = jnp.repeat(layer_depth, field_count)[None, :]
    depth = jnp.where(column % field_count == 0, depth, 0.0)
    share = jnp.where(to == level, 0.5, jnp.where(to < level, 1.0, 0.0))

    eye = jnp.eye(columns, dtype=BF16)
    inside = jnp.concatenate((eye,) + two_terms(share * depth), axis=0)
    blank = jnp.zeros_like(inside)
    mix = jnp.concatenate(
        [jnp.concatenate(pair, axis=1) for pair in ((inside, blank), (blank, inside))], axis=0
    )
    part = jnp.arange(2 * columns) // columns
    same = part[:, None] == part[None, :]
    every = jnp.where(same, jnp.tile(depth[0], 2)[:, None], 0.0)
    every = jnp.concatenate(two_terms(every), axis=0)
    return mix, every


def sums_of_later(total):
    count = lax.axis_size("lev")
    other = lax.ppermute(total, "lev", [(i, i ^ 1) for i in range(count)])
    both = total + other
    later = [
        lax.ppermute(both, "lev", [(i, (i - step) % count) for i in range(count)])
        for step in range(2, count, 2)
    ]
    return other, later


def on_device(fourier, owner, legendre, quad_weights, layer_depth):
    lat_rows, level_count, field_count, doubled = fourier.shape
    waves = doubled // 2
    slots = legendre.shape[0]
    degrees = 2 * legendre.shape[2]
    blocks = waves // slots
    place = lax.axis_index("wave")
    mine = place * slots + jnp.arange(slots, dtype=jnp.int32)
    wave_ids = jnp.arange(waves, dtype=jnp.int32)
    my_waves = jnp.sum(jnp.where(owner[None, :] == mine[:, None], wave_ids[None, :], 0), axis=1)
    lengths = degrees - my_waves * degrees // waves
    lines = jnp.concatenate([quad_weights, lengths.astype(F32), jnp.zeros((8 - slots,), F32)])
    weight = jnp.broadcast_to(lines[:, None], (lines.shape[0], doubled))
    mix, every = level_sums(layer_depth, field_count)
    both = jnp.concatenate([owner, owner + waves])
    order = (both[None, :] == jnp.arange(doubled)[:, None]).astype(BF16)

    outgoing = pack(fourier, owner)
    arrived = lax.all_to_all(outgoing, "wave", split_axis=0, concat_axis=0, tiled=True)
    arrived = arrived.reshape(blocks, slots, lat_rows, doubled)
    results = legendre_pair(arrived, legendre, weight)
    results = results.reshape(waves, lat_rows, doubled)
    returned = lax.all_to_all(results, "wave", split_axis=0, concat_axis=0, tiled=True)
    other, later = sums_of_later(totals(returned, every))
    fields, inside = unpack(returned, owner, mix, level_count)
    fields_out = fields.reshape(fourier.shape)
    geopotential = finish(order, inside, other, later)
    return (fields_out, geopotential)


def solution(mesh):
    return jax.shard_map(
        on_device,
        mesh=mesh,
        in_specs=(P("wave", "lev", None, None), P(), P("wave", None, None, None), P(), P("lev")),
        out_specs=(P("wave", "lev", None, None), P("wave", "lev", None)),
        check_vma=False,
    )
```
